32 devices in a mesh: groups: 2 (over x), port: 16 (over z, y, core).
Axes of the slice: x: 2, y: 2, z: 4, core: 2. Of those that a mesh axis runs over, the one named last changes fastest.
Arguments:
- measured: bfloat16 [4, 2, 4096, 4096], P('groups', None, 'port'), parts along dimension 0, may hold values from -6 to 6
- out_factor: bfloat16 [4096, 1024], P('port', 'groups'), parts along dimension 1, may hold values from -0.25 to 0.25
- in_factor: bfloat16 [1024, 4096], P('groups', 'port'), parts along dimension 0, may hold values from -6 to 6
- pole_rates: float32 [1024], P('groups'), parts along dimension 0, may hold values from 0.1 to 10
- freq_index: int32 [4], P('groups'), parts along dimension 0, may hold values from 0 to 1023
- quad_codes: int32 [4], P('groups'), parts along dimension 0, may hold values from 1 to 4
Outputs:
- grad_out: float32 [4096, 1024], P('port', 'groups'), parts along dimension 1
- grad_in_t: float32 [4096, 1024], P('port', 'groups'), parts along dimension 1
The draws below stay inside these ranges and needn't reach their ends.
There are 2 independent parts, one for each index of `groups`. The reference program is written for one: setup_inputs(seed, part) draws one part's arguments, and reference() takes and returns one part's arrays. A program takes and returns all parts, laid end to end along the dimension named above; each array names one. Nothing has to cross between parts.
All inputs are finite; a program needn't handle non-finite values.
Results may differ from the reference program's by a relative error of at most 0.002.
Values may be sent and summed in bfloat16 or wider, within the bound.
A program may use at most 64 MiB of HBM per device.

```python
import math
import jax
import jax.numpy as jnp

P_OUT = 4096
P_IN = 4096
NP = 512
F = 2
GRID = 1024


def block_scale(stream_key, dims, shards, least, top_value):
    loudness, own = 1.0, jax.random.fold_in(stream_key, 6)
    for axis_at, blocks in shards:
        steps = jnp.exp(jax.random.uniform(jax.random.fold_in(own, axis_at), (blocks,), jnp.float32, least / len(shards), top_value / len(shards)))
        loudness = loudness * jnp.repeat(steps, dims[axis_at] // blocks).reshape([-1 if axis == axis_at else 1 for axis in range(len(dims))])
    return loudness


def bell_draw(own_key, shape, spread, limit, cuts=(), dtype=jnp.bfloat16):
    entries = spread * jax.random.normal(own_key, shape, jnp.float32)
    if cuts:
        entries = entries * block_scale(own_key, shape, cuts, -0.22, 0.18)
    return jnp.clip(entries, -limit, limit).astype(dtype)


def setup_inputs(seed: int = 0, part: int = 0) -> dict:
    arg_keys = jax.random.split(jax.random.key(seed), 7)
    own_keys = jax.random.split(jax.random.fold_in(arg_keys[6], part), 7)
    return {
        "measured": bell_draw(own_keys[0], (F, 2, P_OUT, P_IN), 1.0, 6.0, ((2, 16),)),
        "out_factor": bell_draw(own_keys[1], (P_OUT, NP), NP ** -0.5, 0.25, ((0, 16),)),
        "in_factor": bell_draw(own_keys[2], (NP, P_IN), 1.0, 6.0, ((1, 16),)),
        "pole_rates": jnp.clip(jnp.exp(jax.random.uniform(own_keys[3], (NP,), jnp.float32, math.log(0.1), math.log(10.0))), 0.1, 10.0),
        "freq_index": jax.random.randint(own_keys[4], (F,), 0, GRID).astype(jnp.int32),
        "quad_codes": jax.random.randint(own_keys[5], (F,), 1, 5).astype(jnp.int32),
    }


low_freq = 0.1
log_span = math.log(100.0)


def pole_terms(freq_index, pole_rates):
    omega = low_freq * jnp.exp(log_span * freq_index.astype(jnp.float32) / (GRID - 1))
    denominator = pole_rates[None, :] * pole_rates[None, :] + omega[:, None] * omega[:, None]
    real_side = pole_rates[None, :] / denominator
    imag_side = -omega[:, None] / denominator
    return jnp.stack([real_side, imag_side], axis=1)


def reference(measured, out_factor, in_factor, pole_rates, freq_index, quad_codes):
    coefficients = pole_terms(freq_index, pole_rates)
    weights = quad_codes.astype(jnp.float32) * 0.25
    grad_out = jnp.zeros((P_OUT, NP), jnp.float32)
    grad_in_t = jnp.zeros((P_IN, NP), jnp.float32)
    for freq_slot in range(F):
        for comp_slot in range(2):
            column_scale = coefficients[freq_slot, comp_slot]
            scaled = (out_factor.astype(jnp.float32) * column_scale[None, :]).astype(jnp.bfloat16)
            model = jnp.dot(scaled, in_factor, preferred_element_type=jnp.float32)
            residual = (model - measured[freq_slot, comp_slot].astype(jnp.float32)).astype(jnp.bfloat16)
            factor = weights[freq_slot] * column_scale
            grad_out = grad_out + factor[None, :] * jnp.dot(residual, in_factor.T, preferred_element_type=jnp.float32)
            grad_in_t = grad_in_t + factor[None, :] * jnp.dot(residual.T, out_factor, preferred_element_type=jnp.float32)
    return grad_out * (P_IN ** -0.5), grad_in_t * (P_OUT ** -0.5)
```

```python
import functools
import math

import jax
import jax.numpy as jnp
from jax import lax
from jax.experimental import pallas as pl
from jax.experimental.pallas import tpu as pltpu
from jax.sharding import PartitionSpec as P

GRID = 1024
MESH = pl.DeviceIdType.MESH
RS_TYPE = jnp.float32

low_freq = 0.1
log_span = math.log(100.0)


def contract_second(left, right):
    return lax.dot_general(
        left, right, (((1,), (1,)), ((), ())), preferred_element_type=jnp.float32
    )


def contract_first(left, right):
    return lax.dot_general(
        left, right, (((0,), (0,)), ((), ())), preferred_element_type=jnp.float32
    )


def pole_terms(freq_index, pole_rates):
    omega = low_freq * jnp.exp(log_span * freq_index.astype(jnp.float32) / (GRID - 1))
    denominator = pole_rates[None, :] * pole_rates[None, :] + omega[:, None] * omega[:, None]
    real_side = pole_rates[None, :] / denominator
    imag_side = -omega[:, None] / denominator
    return jnp.stack([real_side, imag_side], axis=1)


def kernel(
    chips, total_out, total_in,
    measured, out_factor, in_factor, rates, freq, quad,
    grad_out, grad_in,
    own, sib_b, meas, scaled, out_t, w_row, w_col, acc, g_own, g_send, g_recv, rs_send, rs_recv,
    loc_sem, meas_sem, ag_s, ag_r, sb_s, sb_r, gs_s, gs_r, rs_s, rs_r,
):
    combos = scaled.shape[0]
    rows, poles = out_factor.shape
    cols = in_factor.shape[1]
    half = chips // 2

    def chip_at(place):
        upper = place // half
        return (1 - upper) * (2 * place) + upper * (2 * (chips - 1 - place) + 1)

    me = lax.axis_index("port")
    core = me % 2
    chip = me // 2
    row_y = chip % 2
    col_z = chip // 2
    place = (1 - row_y) * col_z + row_y * (chips - 1 - col_z)
    sign = 1 - 2 * core
    nxt = chip_at((place + sign + chips) % chips) * 2 + core
    prv = chip_at((place - sign + chips) % chips) * 2 + core
    sib = chip * 2 + 1 - core

    local = pltpu.make_async_copy(in_factor, own.at[0], loc_sem)
    local.start()

    def meas_copy(which, step):
        if which == 0:
            block = chip_at((place - step * sign + chips) % chips) * 2 + core
        else:
            block = chip_at((place + step * sign + chips) % chips) * 2 + 1 - core
        first = pl.multiple_of(block * cols, cols)
        return pltpu.make_async_copy(
            measured.at[:, :, pl.ds(first, cols)], meas.at[which, step], meas_sem.at[which, step]
        )

    barrier = pltpu.get_barrier_semaphore()
    for other in (nxt, prv, sib):
        pl.semaphore_signal(barrier, inc=1, device_id={"port": other}, device_id_type=MESH)

    def remote(src, dst, send, recv, target):
        return pltpu.make_async_remote_copy(
            src_ref=src, dst_ref=dst, send_sem=send, recv_sem=recv,
            device_id={"port": target}, device_id_type=MESH,
        )

    def ag_copy(step):
        return remote(own.at[step], own.at[step + 1], ag_s.at[step], ag_r.at[step + 1], nxt)

    def ag_arrival(step):
        return remote(own.at[step], own.at[step], ag_s.at[step], ag_r.at[step], nxt)

    def sb_copy(step):
        return remote(own.at[step], sib_b.at[step], sb_s.at[step], sb_r.at[step], sib)

    def gs_copy(step):
        return remote(g_send.at[step], g_recv.at[step], gs_s.at[step], gs_r.at[step], sib)

    def rs_copy(step):
        return remote(rs_send.at[step], rs_recv.at[step + 1], rs_s.at[step], rs_r.at[step + 1], nxt)

    def rs_arrival(step):
        return remote(rs_recv.at[step], rs_recv.at[step], rs_s.at[step], rs_r.at[step], nxt)

    pl.semaphore_wait(barrier, 3)
    local.wait()
    ag_copy(0).start()
    sb_copy(0).start()

    @pl.loop(0, chips)
    def _(step):
        meas_copy(0, step).start()
        meas_copy(1, step).start()

    rate = rates[...]
    factor = out_factor[...].astype(jnp.float32)
    out_t[...] = factor.T.astype(jnp.bfloat16)
    for slot in range(combos // 2):
        omega = low_freq * jnp.exp(
            log_span * freq[slot : slot + 1, :].astype(jnp.float32) / (GRID - 1)
        )
        weight = quad[slot : slot + 1, :].astype(jnp.float32) * 0.25
        denominator = rate * rate + omega * omega
        for part, coef in enumerate((rate / denominator, -omega / denominator)):
            k = 2 * slot + part
            scaled[k] = (factor * coef).astype(jnp.bfloat16)
            w_row[k] = jnp.broadcast_to(weight * coef, (8, poles))
            w_col[k] = jnp.broadcast_to(weight * coef, (128, poles)).T
            acc[k] = jnp.zeros((rows, poles), jnp.float32)

    def handle_gather(step):
        ag_arrival(step).wait_recv()

        @pl.when(step < chips - 1)
        def _():
            ag_copy(step).start()

        sb_copy(step).start()

    def compute(step):
        sb_copy(step).wait_recv()
        meas_copy(0, step).wait()
        meas_copy(1, step).wait()
        left = own[step]
        right = sib_b[step]
        gin_own = None
        gin_sib = None
        for k in range(combos):
            stretched = jnp.concatenate([w_col[k]] * (cols // 128), axis=1)
            lhs = scaled[k]
            model = jnp.dot(lhs, left, preferred_element_type=jnp.float32)
            res_own = (model - meas[0, step, k].astype(jnp.float32)).astype(jnp.bfloat16)
            model = jnp.dot(lhs, right, preferred_element_type=jnp.float32)
            res_sib = (model - meas[1, step, k].astype(jnp.float32)).astype(jnp.bfloat16)
            acc[k] += contract_second(res_own, left) + contract_second(res_sib, right)
            transposed = out_t[...]
            part = stretched * jnp.dot(transposed, res_own, preferred_element_type=jnp.float32)
            gin_own = part if gin_own is None else gin_own + part
            part = stretched * jnp.dot(transposed, res_sib, preferred_element_type=jnp.float32)
            gin_sib = part if gin_sib is None else gin_sib + part
        g_send[step] = gin_sib
        gs_copy(step).start()
        g_own[step] = gin_own

    def handle_sum(step):
        gs_copy(step).wait_recv()

        @pl.when(step == 1)
        def _():
            rs_send[step] = (g_own[step] + g_recv[step]).astype(RS_TYPE)

        @pl.when(step > 1)
        def _():
            rs_arrival(step).wait_recv()
            rs_send[step] = (
                g_own[step] + g_recv[step] + rs_recv[step].astype(jnp.float32)
            ).astype(RS_TYPE)

        @pl.when(step > 0)
        def _():
            rs_copy(step).start()

    @pl.loop(0, chips)
    def _(step):
        @pl.when((step > 0) & (step < chips - 1))
        def _():
            handle_gather(step + 1)

        compute(step)

        @pl.when(step == 0)
        def _():
            handle_gather(step + 1)

        @pl.when(step > 0)
        def _():
            handle_sum(step - 1)

    handle_sum(chips - 1)

    total = jnp.zeros((rows, poles), jnp.float32)
    for k in range(combos):
        total = total + w_row[k][0:1, :] * acc[k]
    grad_out[...] = total * (1.0 / math.sqrt(total_in))

    rs_arrival(chips).wait_recv()
    summed = g_own[0] + g_recv[0] + rs_recv[chips].astype(jnp.float32)
    grad_in[...] = (summed * (1.0 / math.sqrt(total_out))).T

    @pl.loop(0, chips)
    def _(step):
        sb_copy(step).wait_send()
        gs_copy(step).wait_send()

        @pl.when(step < chips - 1)
        def _():
            ag_copy(step).wait_send()

        @pl.when(step > 0)
        def _():
            rs_copy(step).wait_send()


def fused(measured, out_factor, in_factor, pole_rates, freq_index, quad_codes):
    combos = measured.shape[0] * 2
    rows, poles = out_factor.shape
    cols = in_factor.shape[1]
    total_in = measured.shape[3]
    ports = lax.axis_size("port")
    total_out = rows * ports
    chips = ports // 2
    vmem = pl.BlockSpec(memory_space=pltpu.VMEM)
    anywhere = pl.BlockSpec(memory_space=pl.ANY)
    dma = pltpu.SemaphoreType.DMA
    call = pl.pallas_call(
        functools.partial(kernel, chips, total_out, total_in),
        out_shape=(
            jax.ShapeDtypeStruct((rows, poles), jnp.float32),
            jax.ShapeDtypeStruct((cols, poles), jnp.float32),
        ),
        in_specs=[anywhere, vmem, anywhere, vmem, vmem, vmem],
        out_specs=(vmem, vmem),
        scratch_shapes=[
            pltpu.VMEM((chips, poles, cols), jnp.bfloat16),
            pltpu.VMEM((chips, poles, cols), jnp.bfloat16),
            pltpu.VMEM((2, chips, combos, rows, cols), jnp.bfloat16),
            pltpu.VMEM((combos, rows, poles), jnp.bfloat16),
            pltpu.VMEM((poles, rows), jnp.bfloat16),
            pltpu.VMEM((combos, 8, poles), jnp.float32),
            pltpu.VMEM((combos, poles, 128), jnp.float32),
            pltpu.VMEM((combos, rows, poles), jnp.float32),
            pltpu.VMEM((chips, poles, cols), jnp.float32),
            pltpu.VMEM((chips, poles, cols), jnp.float32),
            pltpu.VMEM((chips, poles, cols), jnp.float32),
            pltpu.VMEM((chips, poles, cols), RS_TYPE),
            pltpu.VMEM((chips + 1, poles, cols), RS_TYPE),
            dma,
            dma((2, chips)),
            dma((chips,)),
            dma((chips + 1,)),
            dma((chips,)),
            dma((chips,)),
            dma((chips,)),
            dma((chips,)),
            dma((chips + 1,)),
            dma((chips + 1,)),
        ],
        compiler_params=pltpu.CompilerParams(
            collective_id=0, has_side_effects=True, vmem_limit_bytes=60 * 1024 * 1024
        ),
    )
    return call(
        measured.reshape(combos, rows, total_in),
        out_factor,
        in_factor,
        pole_rates.reshape(1, poles),
        freq_index.reshape(-1, 1),
        quad_codes.reshape(-1, 1),
    )


def plain(measured, out_factor, in_factor, pole_rates, freq_index, quad_codes):
    freq_count = measured.shape[0]
    local_rows, pole_count = out_factor.shape
    local_cols = in_factor.shape[1]
    total_in = measured.shape[3]
    total_out = local_rows * lax.axis_size("port")
    coefficients = pole_terms(freq_index, pole_rates)
    weights = quad_codes.astype(jnp.float32) * 0.25
    weighted = weights[:, None, None] * coefficients
    scaled = (
        out_factor.astype(jnp.float32)[None, None, :, :] * coefficients[:, :, None, :]
    ).astype(jnp.bfloat16)
    block_cols = lax.all_gather(in_factor, "port", axis=1, tiled=True)
    width_cols = block_cols.shape[1]
    model = jnp.dot(scaled.reshape(-1, pole_count), block_cols, preferred_element_type=jnp.float32)
    model = model.reshape(freq_count, 2, local_rows, width_cols)
    residual = (model - measured.astype(jnp.float32)).astype(jnp.bfloat16)
    update = contract_second(residual.reshape(-1, width_cols), block_cols)
    update = update.reshape(freq_count, 2, local_rows, pole_count)
    grad_out = jnp.sum(weighted[:, :, None, :] * update, axis=(0, 1))
    grad_out = grad_out * (1.0 / math.sqrt(total_in))
    running = jnp.zeros((width_cols, pole_count), jnp.float32)
    for freq_slot in range(freq_count):
        for comp_slot in range(2):
            running = running + weighted[freq_slot, comp_slot][None, :] * contract_first(
                residual[freq_slot, comp_slot], out_factor
            )
    grad_in_t = lax.psum_scatter(running, "port", scatter_dimension=0, tiled=True)
    return (grad_out, grad_in_t * (1.0 / math.sqrt(total_out)))


def on_device(measured, out_factor, in_factor, pole_rates, freq_index, quad_codes):
    whole_lanes = in_factor.shape[1] % 128 == 0 and out_factor.shape[1] % 128 == 0
    body = fused if whole_lanes and lax.axis_size("port") % 8 == 0 else plain
    return body(measured, out_factor, in_factor, pole_rates, freq_index, quad_codes)


def solution(mesh):
    in_specs = (
        P("groups", None, "port", None),
        P("port", "groups"),
        P("groups", "port"),
        P("groups"),
        P("groups"),
        P("groups"),
    )
    out_specs = (P("port", "groups"), P("port", "groups"))
    return jax.shard_map(
        on_device, mesh=mesh, in_specs=in_specs, out_specs=out_specs, check_vma=False
    )
```

```python
import functools
import math

import jax
import jax.numpy as jnp
from jax import lax
from jax.experimental import pallas as pl
from jax.experimental.pallas import tpu as pltpu
from jax.sharding import PartitionSpec as P

GRID = 1024
MESH = pl.DeviceIdType.MESH
CODE = 16

low_freq = 0.1
log_span = math.log(100.0)


def contract_second(left, right):
    return lax.dot_general(
        left, right, (((1,), (1,)), ((), ())), preferred_element_type=jnp.float32
    )


def contract_first(left, right):
    return lax.dot_general(
        left, right, (((0,), (0,)), ((), ())), preferred_element_type=jnp.float32
    )


def pole_terms(freq_index, pole_rates):
    omega = low_freq * jnp.exp(log_span * freq_index.astype(jnp.float32) / (GRID - 1))
    denominator = pole_rates[None, :] * pole_rates[None, :] + omega[:, None] * omega[:, None]
    real_side = pole_rates[None, :] / denominator
    imag_side = -omega[:, None] / denominator
    return jnp.stack([real_side, imag_side], axis=1)


def kernel(
    chips,
    measured, out_factor, in_factor, rates, freq, quad,
    grad_out, grad_in,
    own, sib_b, meas, scaled, out_t, w_row, w_col, acc, g_own, g_send, g_recv, rs_send, rs_recv,
    loc_sem, meas_sem, ag_s, ag_r, sb_s, sb_r, gs_s, gs_r, rs_s, rs_r,
):
    combos = scaled.shape[0]
    rows, poles = out_factor.shape
    cols = in_factor.shape[1]
    half = chips // 2

    def chip_at(place):
        upper = place // half
        return (1 - upper) * (2 * place) + upper * (2 * (chips - 1 - place) + 1)

    me = lax.axis_index("port")
    core = me % 2
    chip = me // 2
    row_y = chip % 2
    col_z = chip // 2
    place = (1 - row_y) * col_z + row_y * (chips - 1 - col_z)
    sign = 1 - 2 * core
    nxt = chip_at((place + sign + chips) % chips) * 2 + core
    prv = chip_at((place - sign + chips) % chips) * 2 + core
    sib = chip * 2 + 1 - core

    local = pltpu.make_async_copy(in_factor, own.at[0], loc_sem)
    local.start()

    def meas_copy(which, step):
        if which == 0:
            block = chip_at((place - step * sign + chips) % chips) * 2 + core
        else:
            block = chip_at((place + step * sign + chips) % chips) * 2 + 1 - core
        first = pl.multiple_of(block * cols, cols)
        return pltpu.make_async_copy(
            measured.at[:, :, pl.ds(first, cols)], meas.at[which, step], meas_sem.at[which, step]
        )

    barrier = pltpu.get_barrier_semaphore()
    for other in (nxt, prv, sib):
        pl.semaphore_signal(barrier, inc=1, device_id={"port": other}, device_id_type=MESH)

    def remote(src, dst, send, recv, target):
        return pltpu.make_async_remote_copy(
            src_ref=src, dst_ref=dst, send_sem=send, recv_sem=recv,
            device_id={"port": target}, device_id_type=MESH,
        )

    def ag_copy(step):
        return remote(own.at[step], own.at[step + 1], ag_s.at[step], ag_r.at[step + 1], nxt)

    def ag_arrival(step):
        return remote(own.at[step], own.at[step], ag_s.at[step], ag_r.at[step], nxt)

    def sb_copy(step):
        return remote(own.at[step], sib_b.at[step], sb_s.at[step], sb_r.at[step], sib)

    def gs_copy(step):
        return remote(g_send.at[step], g_recv.at[step], gs_s.at[step], gs_r.at[step], sib)

    def rs_copy(step):
        return remote(rs_send.at[step], rs_recv.at[step + 1], rs_s.at[step], rs_r.at[step + 1], nxt)

    def rs_arrival(step):
        return remote(rs_recv.at[step], rs_recv.at[step], rs_s.at[step], rs_r.at[step], nxt)

    pl.semaphore_wait(barrier, 3)
    local.wait()
    ag_copy(0).start()
    sb_copy(0).start()

    @pl.loop(0, chips)
    def _(step):
        meas_copy(0, step).start()
        meas_copy(1, step).start()

    rate = rates[...]
    factor = out_factor[...].astype(jnp.float32)
    out_t[...] = factor.T.astype(jnp.bfloat16)
    for slot in range(combos // 2):
        position = jnp.full((1, poles), freq[slot], jnp.int32).astype(jnp.float32)
        omega = low_freq * jnp.exp(log_span * position / (GRID - 1))
        weight = jnp.full((1, poles), quad[slot], jnp.int32).astype(jnp.float32) * 0.25
        denominator = rate * rate + omega * omega
        for part, coef in enumerate((rate / denominator, -omega / denominator)):
            k = 2 * slot + part
            scaled[k] = (factor * coef).astype(jnp.bfloat16)
            w_row[k] = jnp.broadcast_to(weight * coef, (8, poles))
            w_col[k] = jnp.broadcast_to(weight * coef, (128, poles)).T
            acc[k] = jnp.zeros((rows, poles), jnp.float32)

    def handle_gather(step):
        ag_arrival(step).wait_recv()

        @pl.when(step < chips - 1)
        def _():
            ag_copy(step).start()

        sb_copy(step).start()

    def compute(step):
        sb_copy(step).wait_recv()
        meas_copy(0, step).wait()
        meas_copy(1, step).wait()
        left = own[step]
        right = sib_b[step]
        gin_own = None
        gin_sib = None
        for k in range(combos):
            stretched = jnp.concatenate([w_col[k]] * (cols // 128), axis=1)
            lhs = scaled[k]
            model = jnp.dot(lhs, left, preferred_element_type=jnp.float32)
            res_own = (model - meas[0, step, k].astype(jnp.float32)).astype(jnp.bfloat16)
            model = jnp.dot(lhs, right, preferred_element_type=jnp.float32)
            res_sib = (model - meas[1, step, k].astype(jnp.float32)).astype(jnp.bfloat16)
            acc[k] += contract_second(res_own, left) + contract_second(res_sib, right)
            transposed = out_t[...]
            part = stretched * jnp.dot(transposed, res_own, preferred_element_type=jnp.float32)
            gin_own = part if gin_own is None else gin_own + part
            part = stretched * jnp.dot(transposed, res_sib, preferred_element_type=jnp.float32)
            gin_sib = part if gin_sib is None else gin_sib + part
        g_send[step] = gin_sib
        gs_copy(step).start()
        g_own[step] = gin_own

    def encode(step, value):
        largest = jnp.maximum(jnp.max(jnp.abs(value), axis=0, keepdims=True), 1e-30)
        exponent = jnp.ceil(jnp.log2(largest) + 0.01) - 15.0
        coded = jnp.round(value * jnp.exp2(-exponent))
        rs_send[step, :poles, :] = coded.astype(jnp.int32).astype(jnp.int16)
        tail = jnp.broadcast_to(exponent.astype(jnp.int32), (CODE, cols))
        rs_send[step, poles:, :] = tail.astype(jnp.int16)

    def decode(step):
        tail = rs_recv[step, poles:, :].astype(jnp.int32).astype(jnp.float32)
        return rs_recv[step, :poles, :].astype(jnp.int32).astype(jnp.float32) * jnp.exp2(tail[0:1])

    def handle_sum(step):
        gs_copy(step).wait_recv()

        @pl.when(step == 1)
        def _():
            encode(step, g_own[step] + g_recv[step])

        @pl.when(step > 1)
        def _():
            rs_arrival(step).wait_recv()
            encode(step, g_own[step] + g_recv[step] + decode(step))

        @pl.when(step > 0)
        def _():
            rs_copy(step).start()

    @pl.loop(0, chips)
    def _(step):
        @pl.when((step > 0) & (step < chips - 1))
        def _():
            handle_gather(step + 1)

        compute(step)

        @pl.when(step == 0)
        def _():
            handle_gather(step + 1)

        @pl.when(step > 0)
        def _():
            handle_sum(step - 1)

    handle_sum(chips - 1)

    total = jnp.zeros((rows, poles), jnp.float32)
    for k in range(combos):
        total = total + w_row[k][0:1, :] * acc[k]
    grad_out[...] = total

    rs_arrival(chips).wait_recv()
    summed = g_own[0] + g_recv[0] + decode(chips)
    grad_in[...] = summed.T

    @pl.loop(0, chips)
    def _(step):
        sb_copy(step).wait_send()
        gs_copy(step).wait_send()

        @pl.when(step < chips - 1)
        def _():
            ag_copy(step).wait_send()

        @pl.when(step > 0)
        def _():
            rs_copy(step).wait_send()


def fused(measured, out_factor, in_factor, pole_rates, freq_index, quad_codes):
    combos = measured.shape[0] * 2
    rows, poles = out_factor.shape
    cols = in_factor.shape[1]
    total_in = measured.shape[3]
    ports = lax.axis_size("port")
    total_out = rows * ports
    chips = ports // 2
    vmem = pl.BlockSpec(memory_space=pltpu.VMEM)
    anywhere = pl.BlockSpec(memory_space=pl.ANY)
    scalar = pl.BlockSpec(memory_space=pltpu.SMEM)
    dma = pltpu.SemaphoreType.DMA
    call = pl.pallas_call(
        functools.partial(kernel, chips),
        out_shape=(
            jax.ShapeDtypeStruct((rows, poles), jnp.float32),
            jax.ShapeDtypeStruct((cols, poles), jnp.float32),
        ),
        in_specs=[anywhere, vmem, anywhere, vmem, scalar, scalar],
        out_specs=(vmem, vmem),
        scratch_shapes=[
            pltpu.VMEM((chips, poles, cols), jnp.bfloat16),
            pltpu.VMEM((chips, poles, cols), jnp.bfloat16),
            pltpu.VMEM((2, chips, combos, rows, cols), jnp.bfloat16),
            pltpu.VMEM((combos, rows, poles), jnp.bfloat16),
            pltpu.VMEM((poles, rows), jnp.bfloat16),
            pltpu.VMEM((combos, 8, poles), jnp.float32),
            pltpu.VMEM((combos, poles, 128), jnp.float32),
            pltpu.VMEM((combos, rows, poles), jnp.float32),
            pltpu.VMEM((chips, poles, cols), jnp.float32),
            pltpu.VMEM((chips, poles, cols), jnp.float32),
            pltpu.VMEM((chips, poles, cols), jnp.float32),
            pltpu.VMEM((chips, poles + CODE, cols), jnp.int16),
            pltpu.VMEM((chips + 1, poles + CODE, cols), jnp.int16),
            dma,
            dma((2, chips)),
            dma((chips,)),
            dma((chips + 1,)),
            dma((chips,)),
            dma((chips,)),
            dma((chips,)),
            dma((chips,)),
            dma((chips + 1,)),
            dma((chips + 1,)),
        ],
        compiler_params=pltpu.CompilerParams(
            collective_id=0, has_side_effects=True, vmem_limit_bytes=60 * 1024 * 1024
        ),
    )
    grad_out, grad_in = call(
        measured.reshape(combos, rows, total_in),
        out_factor,
        in_factor,
        pole_rates.reshape(1, poles),
        freq_index,
        quad_codes,
    )
    return grad_out * (1.0 / math.sqrt(total_in)), grad_in * (1.0 / math.sqrt(total_out))


def plain(measured, out_factor, in_factor, pole_rates, freq_index, quad_codes):
    freq_count = measured.shape[0]
    local_rows, pole_count = out_factor.shape
    local_cols = in_factor.shape[1]
    total_in = measured.shape[3]
    total_out = local_rows * lax.axis_size("port")
    coefficients = pole_terms(freq_index, pole_rates)
    weights = quad_codes.astype(jnp.float32) * 0.25
    weighted = weights[:, None, None] * coefficients
    scaled = (
        out_factor.astype(jnp.float32)[None, None, :, :] * coefficients[:, :, None, :]
    ).astype(jnp.bfloat16)
    block_cols = lax.all_gather(in_factor, "port", axis=1, tiled=True)
    width_cols = block_cols.shape[1]
    model = jnp.dot(scaled.reshape(-1, pole_count), block_cols, preferred_element_type=jnp.float32)
    model = model.reshape(freq_count, 2, local_rows, width_cols)
    residual = (model - measured.astype(jnp.float32)).astype(jnp.bfloat16)
    update = contract_second(residual.reshape(-1, width_cols), block_cols)
    update = update.reshape(freq_count, 2, local_rows, pole_count)
    grad_out = jnp.sum(weighted[:, :, None, :] * update, axis=(0, 1))
    grad_out = grad_out * (1.0 / math.sqrt(total_in))
    running = jnp.zeros((width_cols, pole_count), jnp.float32)
    for freq_slot in range(freq_count):
        for comp_slot in range(2):
            running = running + weighted[freq_slot, comp_slot][None, :] * contract_first(
                residual[freq_slot, comp_slot], out_factor
            )
    grad_in_t = lax.psum_scatter(running, "port", scatter_dimension=0, tiled=True)
    return (grad_out, grad_in_t * (1.0 / math.sqrt(total_out)))


def on_device(measured, out_factor, in_factor, pole_rates, freq_index, quad_codes):
    whole_lanes = in_factor.shape[1] % 128 == 0 and out_factor.shape[1] % 128 == 0
    body = fused if whole_lanes and lax.axis_size("port") % 8 == 0 else plain
    return body(measured, out_factor, in_factor, pole_rates, freq_index, quad_codes)


def solution(mesh):
    in_specs = (
        P("groups", None, "port", None),
        P("port", "groups"),
        P("groups", "port"),
        P("groups"),
        P("groups"),
        P("groups"),
    )
    out_specs = (P("port", "groups"), P("port", "groups"))
    return jax.shard_map(
        on_device, mesh=mesh, in_specs=in_specs, out_specs=out_specs, check_vma=False
    )
```

```python
import functools
import math

import jax
import jax.numpy as jnp
from jax import lax
from jax.experimental import pallas as pl
from jax.experimental.pallas import tpu as pltpu
from jax.sharding import PartitionSpec as P

GRID = 1024
MESH = pl.DeviceIdType.MESH
CODE = 16
PIECES = 2

low_freq = 0.1
log_span = math.log(100.0)


def contract_second(left, right):
    return lax.dot_general(
        left, right, (((1,), (1,)), ((), ())), preferred_element_type=jnp.float32
    )


def contract_first(left, right):
    return lax.dot_general(
        left, right, (((0,), (0,)), ((), ())), preferred_element_type=jnp.float32
    )


def pole_terms(freq_index, pole_rates):
    omega = low_freq * jnp.exp(log_span * freq_index.astype(jnp.float32) / (GRID - 1))
    denominator = pole_rates[None, :] * pole_rates[None, :] + omega[:, None] * omega[:, None]
    real_side = pole_rates[None, :] / denominator
    imag_side = -omega[:, None] / denominator
    return jnp.stack([real_side, imag_side], axis=1)


def kernel(
    chips,
    measured, out_factor, in_factor, rates, freq, quad,
    grad_out, grad_in,
    own, sib_b, meas, scaled, out_t, w_row, w_col, acc, g_own, g_send, g_recv, rs_send, rs_recv,
    loc_sem, meas_sem, ag_s, ag_r, sb_s, sb_r, gs_s, gs_r, rs_s, rs_r,
):
    combos = scaled.shape[0]
    rows, poles = out_factor.shape
    cols = in_factor.shape[1]
    half = chips // 2

    def chip_at(place):
        upper = place // half
        return (1 - upper) * (2 * place) + upper * (2 * (chips - 1 - place) + 1)

    me = lax.axis_index("port")
    core = me % 2
    chip = me // 2
    row_y = chip % 2
    col_z = chip // 2
    place = (1 - row_y) * col_z + row_y * (chips - 1 - col_z)
    sign = 1 - 2 * core
    nxt = chip_at((place + sign + chips) % chips) * 2 + core
    prv = chip_at((place - sign + chips) % chips) * 2 + core
    sib = chip * 2 + 1 - core

    local = pltpu.make_async_copy(in_factor, own.at[0], loc_sem)
    local.start()

    def meas_copy(which, step):
        if which == 0:
            block = chip_at((place - step * sign + chips) % chips) * 2 + core
        else:
            block = chip_at((place + step * sign + chips) % chips) * 2 + 1 - core
        first = pl.multiple_of(block * cols, cols)
        return pltpu.make_async_copy(
            measured.at[:, :, pl.ds(first, cols)], meas.at[which, step], meas_sem.at[which, step]
        )

    barrier = pltpu.get_barrier_semaphore()
    for other in (nxt, prv, sib):
        pl.semaphore_signal(barrier, inc=1, device_id={"port": other}, device_id_type=MESH)

    def remote(src, dst, send, recv, target):
        return pltpu.make_async_remote_copy(
            src_ref=src, dst_ref=dst, send_sem=send, recv_sem=recv,
            device_id={"port": target}, device_id_type=MESH,
        )

    share = poles // PIECES

    def ag_copy(step, piece, ahead=1):
        part = pl.ds(piece * share, share)
        return remote(
            own.at[step, part], own.at[step + ahead, part],
            ag_s.at[step, piece], ag_r.at[step + ahead, piece], nxt,
        )

    def ag_arrival(step, piece):
        return ag_copy(step, piece, 0)

    def sb_copy(step):
        return remote(own.at[step], sib_b.at[step], sb_s.at[step], sb_r.at[step], sib)

    def gs_copy(step):
        return remote(g_send.at[step], g_recv.at[step], gs_s.at[step], gs_r.at[step], sib)

    def rs_copy(step, piece):
        return remote(
            rs_send.at[step, piece], rs_recv.at[step + 1, piece],
            rs_s.at[step, piece], rs_r.at[step + 1, piece], nxt,
        )

    def rs_arrival(step, piece):
        return remote(
            rs_recv.at[step, piece], rs_recv.at[step, piece],
            rs_s.at[step, piece], rs_r.at[step, piece], nxt,
        )

    pl.semaphore_wait(barrier, 3)
    local.wait()
    for piece in range(PIECES):
        ag_copy(0, piece).start()
    sb_copy(0).start()

    @pl.loop(0, chips)
    def _(step):
        meas_copy(0, step).start()
        meas_copy(1, step).start()

    rate = rates[...]
    factor = out_factor[...].astype(jnp.float32)
    out_t[...] = factor.T.astype(jnp.bfloat16)
    for slot in range(combos // 2):
        position = jnp.full((1, poles), freq[slot], jnp.int32).astype(jnp.float32)
        omega = low_freq * jnp.exp(log_span * position / (GRID - 1))
        weight = jnp.full((1, poles), quad[slot], jnp.int32).astype(jnp.float32) * 0.25
        denominator = rate * rate + omega * omega
        for part, coef in enumerate((rate / denominator, -omega / denominator)):
            k = 2 * slot + part
            scaled[k] = (factor * coef).astype(jnp.bfloat16)
            w_row[k] = jnp.broadcast_to(weight * coef, (8, poles))
            w_col[k] = jnp.broadcast_to(weight * coef, (128, poles)).T
            acc[k] = jnp.zeros((rows, poles), jnp.float32)

    def handle_gather(step, piece):
        ag_arrival(step, piece).wait_recv()

        @pl.when(step < chips - 1)
        def _():
            ag_copy(step, piece).start()

        if piece == PIECES - 1:
            sb_copy(step).start()

    def compute(step, between):
        sb_copy(step).wait_recv()
        meas_copy(0, step).wait()
        meas_copy(1, step).wait()
        left = own[step]
        right = sib_b[step]
        gin_own = None
        gin_sib = None
        for k in range(combos):
            stretched = jnp.concatenate([w_col[k]] * (cols // 128), axis=1)
            lhs = scaled[k]
            model = jnp.dot(lhs, left, preferred_element_type=jnp.float32)
            res_own = (model - meas[0, step, k].astype(jnp.float32)).astype(jnp.bfloat16)
            model = jnp.dot(lhs, right, preferred_element_type=jnp.float32)
            res_sib = (model - meas[1, step, k].astype(jnp.float32)).astype(jnp.bfloat16)
            acc[k] += contract_second(res_own, left) + contract_second(res_sib, right)
            transposed = out_t[...]
            part = stretched * jnp.dot(transposed, res_own, preferred_element_type=jnp.float32)
            gin_own = part if gin_own is None else gin_own + part
            part = stretched * jnp.dot(transposed, res_sib, preferred_element_type=jnp.float32)
            gin_sib = part if gin_sib is None else gin_sib + part
            between(step, k)
        g_send[step] = gin_sib
        gs_copy(step).start()
        g_own[step] = gin_own

    def encode(step, piece, value):
        largest = jnp.maximum(jnp.max(jnp.abs(value), axis=0, keepdims=True), 1e-30)
        exponent = jnp.ceil(jnp.log2(largest) + 0.01) - 15.0
        coded = jnp.round(value * jnp.exp2(-exponent))
        rs_send[step, piece, :share, :] = coded.astype(jnp.int32).astype(jnp.int16)
        tail = jnp.broadcast_to(exponent.astype(jnp.int32), (CODE, cols))
        rs_send[step, piece, share:, :] = tail.astype(jnp.int16)

    def decode(step, piece):
        tail = rs_recv[step, piece, share:, :].astype(jnp.int32).astype(jnp.float32)
        body = rs_recv[step, piece, :share, :].astype(jnp.int32).astype(jnp.float32)
        return body * jnp.exp2(tail[0:1])

    def chip_sum(step, piece):
        part = pl.ds(piece * share, share)
        return g_own[step, part, :] + g_recv[step, part, :]

    def handle_sum(step, piece):
        if piece == 0:
            gs_copy(step).wait_recv()

        @pl.when(step == 1)
        def _():
            encode(step, piece, chip_sum(step, piece))

        @pl.when(step > 1)
        def _():
            rs_arrival(step, piece).wait_recv()
            encode(step, piece, chip_sum(step, piece) + decode(step, piece))

        @pl.when(step > 0)
        def _():
            rs_copy(step, piece).start()

    slots = 2 * PIECES

    def between(step, k):
        for slot in range(k * slots // combos, (k + 1) * slots // combos):
            piece = slot % PIECES
            if slot < PIECES:

                @pl.when(step < chips - 1)
                def _():
                    handle_gather(step + 1, piece)
            else:

                @pl.when(step > 0)
                def _():
                    handle_sum(step - 1, piece)

    @pl.loop(0, chips)
    def _(step):
        compute(step, between)

    for piece in range(PIECES):
        handle_sum(chips - 1, piece)

    total = jnp.zeros((rows, poles), jnp.float32)
    for k in range(combos):
        total = total + w_row[k][0:1, :] * acc[k]
    grad_out[...] = total

    for piece in range(PIECES):
        rs_arrival(chips, piece).wait_recv()
        summed = chip_sum(0, piece) + decode(chips, piece)
        grad_in[:, piece * share : (piece + 1) * share] = summed.T

    @pl.loop(0, chips)
    def _(step):
        sb_copy(step).wait_send()
        gs_copy(step).wait_send()

        for piece in range(PIECES):

            @pl.when(step < chips - 1)
            def _():
                ag_copy(step, piece).wait_send()

            @pl.when(step > 0)
            def _():
                rs_copy(step, piece).wait_send()


def fused(measured, out_factor, in_factor, pole_rates, freq_index, quad_codes):
    combos = measured.shape[0] * 2
    rows, poles = out_factor.shape
    cols = in_factor.shape[1]
    total_in = measured.shape[3]
    ports = lax.axis_size("port")
    total_out = rows * ports
    chips = ports // 2
    vmem = pl.BlockSpec(memory_space=pltpu.VMEM)
    anywhere = pl.BlockSpec(memory_space=pl.ANY)
    scalar = pl.BlockSpec(memory_space=pltpu.SMEM)
    dma = pltpu.SemaphoreType.DMA
    call = pl.pallas_call(
        functools.partial(kernel, chips),
        out_shape=(
            jax.ShapeDtypeStruct((rows, poles), jnp.float32),
            jax.ShapeDtypeStruct((cols, poles), jnp.float32),
        ),
        in_specs=[anywhere, vmem, anywhere, vmem, scalar, scalar],
        out_specs=(vmem, vmem),
        scratch_shapes=[
            pltpu.VMEM((chips, poles, cols), jnp.bfloat16),
            pltpu.VMEM((chips, poles, cols), jnp.bfloat16),
            pltpu.VMEM((2, chips, combos, rows, cols), jnp.bfloat16),
            pltpu.VMEM((combos, rows, poles), jnp.bfloat16),
            pltpu.VMEM((poles, rows), jnp.bfloat16),
            pltpu.VMEM((combos, 8, poles), jnp.float32),
            pltpu.VMEM((combos, poles, 128), jnp.float32),
            pltpu.VMEM((combos, rows, poles), jnp.float32),
            pltpu.VMEM((chips, poles, cols), jnp.float32),
            pltpu.VMEM((chips, poles, cols), jnp.float32),
            pltpu.VMEM((chips, poles, cols), jnp.float32),
            pltpu.VMEM((chips, PIECES, poles // PIECES + CODE, cols), jnp.int16),
            pltpu.VMEM((chips + 1, PIECES, poles // PIECES + CODE, cols), jnp.int16),
            dma,
            dma((2, chips)),
            dma((chips, PIECES)),
            dma((chips + 1, PIECES)),
            dma((chips,)),
            dma((chips,)),
            dma((chips,)),
            dma((chips,)),
            dma((chips + 1, PIECES)),
            dma((chips + 1, PIECES)),
        ],
        compiler_params=pltpu.CompilerParams(
            collective_id=0, has_side_effects=True, vmem_limit_bytes=60 * 1024 * 1024
        ),
    )
    grad_out, grad_in = call(
        measured.reshape(combos, rows, total_in),
        out_factor,
        in_factor,
        pole_rates.reshape(1, poles),
        freq_index,
        quad_codes,
    )
    return grad_out * (1.0 / math.sqrt(total_in)), grad_in * (1.0 / math.sqrt(total_out))


def plain(measured, out_factor, in_factor, pole_rates, freq_index, quad_codes):
    freq_count = measured.shape[0]
    local_rows, pole_count = out_factor.shape
    local_cols = in_factor.shape[1]
    total_in = measured.shape[3]
    total_out = local_rows * lax.axis_size("port")
    coefficients = pole_terms(freq_index, pole_rates)
    weights = quad_codes.astype(jnp.float32) * 0.25
    weighted = weights[:, None, None] * coefficients
    scaled = (
        out_factor.astype(jnp.float32)[None, None, :, :] * coefficients[:, :, None, :]
    ).astype(jnp.bfloat16)
    block_cols = lax.all_gather(in_factor, "port", axis=1, tiled=True)
    width_cols = block_cols.shape[1]
    model = jnp.dot(scaled.reshape(-1, pole_count), block_cols, preferred_element_type=jnp.float32)
    model = model.reshape(freq_count, 2, local_rows, width_cols)
    residual = (model - measured.astype(jnp.float32)).astype(jnp.bfloat16)
    update = contract_second(residual.reshape(-1, width_cols), block_cols)
    update = update.reshape(freq_count, 2, local_rows, pole_count)
    grad_out = jnp.sum(weighted[:, :, None, :] * update, axis=(0, 1))
    grad_out = grad_out * (1.0 / math.sqrt(total_in))
    running = jnp.zeros((width_cols, pole_count), jnp.float32)
    for freq_slot in range(freq_count):
        for comp_slot in range(2):
            running = running + weighted[freq_slot, comp_slot][None, :] * contract_first(
                residual[freq_slot, comp_slot], out_factor
            )
    grad_in_t = lax.psum_scatter(running, "port", scatter_dimension=0, tiled=True)
    return (grad_out, grad_in_t * (1.0 / math.sqrt(total_out)))


def on_device(measured, out_factor, in_factor, pole_rates, freq_index, quad_codes):
    whole_lanes = in_factor.shape[1] % 128 == 0 and out_factor.shape[1] % 128 == 0
    body = fused if whole_lanes and lax.axis_size("port") % 8 == 0 else plain
    return body(measured, out_factor, in_factor, pole_rates, freq_index, quad_codes)


def solution(mesh):
    in_specs = (
        P("groups", None, "port", None),
        P("port", "groups"),
        P("groups", "port"),
        P("groups"),
        P("groups"),
        P("groups"),
    )
    out_specs = (P("port", "groups"), P("port", "groups"))
    return jax.shard_map(
        on_device, mesh=mesh, in_specs=in_specs, out_specs=out_specs, check_vma=False
    )
```

```python
import functools
import math

import jax
import jax.numpy as jnp
from jax import lax
from jax.experimental import pallas as pl
from jax.experimental.pallas import tpu as pltpu
from jax.sharding import PartitionSpec as P

GRID = 1024
MESH = pl.DeviceIdType.MESH
CODE = 16
PIECES = 2

low_freq = 0.1
log_span = math.log(100.0)


def contract_second(left, right):
    return lax.dot_general(
        left, right, (((1,), (1,)), ((), ())), preferred_element_type=jnp.float32
    )


def contract_first(left, right):
    return lax.dot_general(
        left, right, (((0,), (0,)), ((), ())), preferred_element_type=jnp.float32
    )


def pole_terms(freq_index, pole_rates):
    omega = low_freq * jnp.exp(log_span * freq_index.astype(jnp.float32) / (GRID - 1))
    denominator = pole_rates[None, :] * pole_rates[None, :] + omega[:, None] * omega[:, None]
    real_side = pole_rates[None, :] / denominator
    imag_side = -omega[:, None] / denominator
    return jnp.stack([real_side, imag_side], axis=1)


def kernel(
    chips,
    measured, out_factor, in_factor, rates, freq, quad,
    grad_out, grad_in,
    own, sib_b, meas, scaled, out_t, w_row, w_col, acc, g_own, g_send, g_recv, rs_send, rs_recv,
    loc_sem, meas_sem, ag_s, ag_r, sb_s, sb_r, gs_s, gs_r, rs_s, rs_r,
):
    combos = scaled.shape[0]
    rows, poles = out_factor.shape
    cols = in_factor.shape[1]
    half = chips // 2

    def chip_at(place):
        upper = place // half
        return (1 - upper) * (2 * place) + upper * (2 * (chips - 1 - place) + 1)

    me = lax.axis_index("port")
    core = me % 2
    chip = me // 2
    row_y = chip % 2
    col_z = chip // 2
    place = (1 - row_y) * col_z + row_y * (chips - 1 - col_z)
    sign = 1 - 2 * core
    nxt = chip_at((place + sign + chips) % chips) * 2 + core
    prv = chip_at((place - sign + chips) % chips) * 2 + core
    sib = chip * 2 + 1 - core

    local = pltpu.make_async_copy(in_factor, own.at[0], loc_sem)
    local.start()

    def meas_copy(which, step):
        if which == 0:
            block = chip_at((place - step * sign + chips) % chips) * 2 + core
        else:
            block = chip_at((place + step * sign + chips) % chips) * 2 + 1 - core
        first = pl.multiple_of(block * cols, cols)
        return pltpu.make_async_copy(
            measured.at[:, :, pl.ds(first, cols)], meas.at[which, step], meas_sem.at[which, step]
        )

    barrier = pltpu.get_barrier_semaphore()
    for other in (nxt, prv, sib):
        pl.semaphore_signal(barrier, inc=1, device_id={"port": other}, device_id_type=MESH)

    def remote(src, dst, send, recv, target):
        return pltpu.make_async_remote_copy(
            src_ref=src, dst_ref=dst, send_sem=send, recv_sem=recv,
            device_id={"port": target}, device_id_type=MESH,
        )

    share = poles // PIECES

    def ag_copy(step, piece, ahead=1):
        part = pl.ds(piece * share, share)
        return remote(
            own.at[step, part], own.at[step + ahead, part],
            ag_s.at[step, piece], ag_r.at[step + ahead, piece], nxt,
        )

    def ag_arrival(step, piece):
        return ag_copy(step, piece, 0)

    def sb_copy(step):
        return remote(own.at[step], sib_b.at[step], sb_s.at[step], sb_r.at[step], sib)

    def gs_copy(step):
        return remote(g_send.at[step], g_recv.at[step], gs_s.at[step], gs_r.at[step], sib)

    def rs_copy(step, piece):
        return remote(
            rs_send.at[step, piece], rs_recv.at[step + 1, piece],
            rs_s.at[step, piece], rs_r.at[step + 1, piece], nxt,
        )

    def rs_arrival(step, piece):
        return remote(
            rs_recv.at[step, piece], rs_recv.at[step, piece],
            rs_s.at[step, piece], rs_r.at[step, piece], nxt,
        )

    pl.semaphore_wait(barrier, 3)
    local.wait()
    for piece in range(PIECES):
        ag_copy(0, piece).start()
    sb_copy(0).start()

    @pl.loop(0, chips)
    def _(step):
        meas_copy(0, step).start()
        meas_copy(1, step).start()

    rate = rates[...]
    factor = out_factor[...].astype(jnp.float32)
    out_t[...] = factor.T.astype(jnp.bfloat16)
    for slot in range(combos // 2):
        position = jnp.full((1, poles), freq[slot], jnp.int32).astype(jnp.float32)
        omega = low_freq * jnp.exp(log_span * position / (GRID - 1))
        weight = jnp.full((1, poles), quad[slot], jnp.int32).astype(jnp.float32) * 0.25
        denominator = rate * rate + omega * omega
        for part, coef in enumerate((rate / denominator, -omega / denominator)):
            k = 2 * slot + part
            scaled[k] = (factor * coef).astype(jnp.bfloat16)
            w_row[k] = jnp.broadcast_to(weight * coef, (8, poles))
            w_col[k] = jnp.broadcast_to(weight * coef, (128, poles)).T
            acc[k] = jnp.zeros((rows, poles), jnp.float32)

    def handle_gather(step, piece):
        ag_arrival(step, piece).wait_recv()

        @pl.when(step < chips - 1)
        def _():
            ag_copy(step, piece).start()

        if piece == PIECES - 1:
            sb_copy(step).start()

    def compute(step, between):
        sb_copy(step).wait_recv()
        meas_copy(0, step).wait()
        meas_copy(1, step).wait()
        left = own[step]
        right = sib_b[step]
        gin_own = None
        gin_sib = None
        for k in range(combos):
            stretched = jnp.concatenate([w_col[k]] * (cols // 128), axis=1)
            lhs = scaled[k]
            model = jnp.dot(lhs, left, preferred_element_type=jnp.float32)
            res_own = (model - meas[0, step, k].astype(jnp.float32)).astype(jnp.bfloat16)
            model = jnp.dot(lhs, right, preferred_element_type=jnp.float32)
            res_sib = (model - meas[1, step, k].astype(jnp.float32)).astype(jnp.bfloat16)
            acc[k] += contract_second(res_own, left) + contract_second(res_sib, right)
            transposed = out_t[...]
            part = stretched * jnp.dot(transposed, res_own, preferred_element_type=jnp.float32)
            gin_own = part if gin_own is None else gin_own + part
            part = stretched * jnp.dot(transposed, res_sib, preferred_element_type=jnp.float32)
            gin_sib = part if gin_sib is None else gin_sib + part
            between(step, k)
        peak = jnp.maximum(jnp.max(jnp.abs(gin_sib), axis=0, keepdims=True), 1e-30)
        power = jnp.ceil(jnp.log2(peak) + 0.01) - 15.0
        coded = jnp.round(gin_sib * jnp.exp2(-power))
        g_send[step, :poles, :] = coded.astype(jnp.int32).astype(jnp.int16)
        ends = jnp.broadcast_to(power.astype(jnp.int32), (CODE, cols))
        g_send[step, poles:, :] = ends.astype(jnp.int16)
        gs_copy(step).start()
        g_own[step] = gin_own

    def encode(step, piece, value):
        largest = jnp.maximum(jnp.max(jnp.abs(value), axis=0, keepdims=True), 1e-30)
        exponent = jnp.ceil(jnp.log2(largest) + 0.01) - 15.0
        coded = jnp.round(value * jnp.exp2(-exponent))
        rs_send[step, piece, :share, :] = coded.astype(jnp.int32).astype(jnp.int16)
        tail = jnp.broadcast_to(exponent.astype(jnp.int32), (CODE, cols))
        rs_send[step, piece, share:, :] = tail.astype(jnp.int16)

    def decode(step, piece):
        tail = rs_recv[step, piece, share:, :].astype(jnp.int32).astype(jnp.float32)
        body = rs_recv[step, piece, :share, :].astype(jnp.int32).astype(jnp.float32)
        return body * jnp.exp2(tail[0:1])

    def chip_sum(step, piece):
        part = pl.ds(piece * share, share)
        ends = g_recv[step, poles:, :].astype(jnp.int32).astype(jnp.float32)
        body = g_recv[step, part, :].astype(jnp.int32).astype(jnp.float32)
        return g_own[step, part, :] + body * jnp.exp2(ends[0:1])

    def handle_sum(step, piece):
        if piece == 0:
            gs_copy(step).wait_recv()

        @pl.when(step == 1)
        def _():
            encode(step, piece, chip_sum(step, piece))

        @pl.when(step > 1)
        def _():
            rs_arrival(step, piece).wait_recv()
            encode(step, piece, chip_sum(step, piece) + decode(step, piece))

        @pl.when(step > 0)
        def _():
            rs_copy(step, piece).start()

    slots = 2 * PIECES

    def between(step, k):
        for slot in range(k * slots // combos, (k + 1) * slots // combos):
            piece = slot % PIECES
            if slot < PIECES:

                @pl.when(step < chips - 1)
                def _():
                    handle_gather(step + 1, piece)
            else:

                @pl.when(step > 0)
                def _():
                    handle_sum(step - 1, piece)

    @pl.loop(0, chips)
    def _(step):
        compute(step, between)

    for piece in range(PIECES):
        handle_sum(chips - 1, piece)

    total = jnp.zeros((rows, poles), jnp.float32)
    for k in range(combos):
        total = total + w_row[k][0:1, :] * acc[k]
    grad_out[...] = total

    for piece in range(PIECES):
        rs_arrival(chips, piece).wait_recv()
        summed = chip_sum(0, piece) + decode(chips, piece)
        grad_in[:, piece * share : (piece + 1) * share] = summed.T

    @pl.loop(0, chips)
    def _(step):
        sb_copy(step).wait_send()
        gs_copy(step).wait_send()

        for piece in range(PIECES):

            @pl.when(step < chips - 1)
            def _():
                ag_copy(step, piece).wait_send()

            @pl.when(step > 0)
            def _():
                rs_copy(step, piece).wait_send()


def fused(measured, out_factor, in_factor, pole_rates, freq_index, quad_codes):
    combos = measured.shape[0] * 2
    rows, poles = out_factor.shape
    cols = in_factor.shape[1]
    total_in = measured.shape[3]
    ports = lax.axis_size("port")
    total_out = rows * ports
    chips = ports // 2
    vmem = pl.BlockSpec(memory_space=pltpu.VMEM)
    anywhere = pl.BlockSpec(memory_space=pl.ANY)
    scalar = pl.BlockSpec(memory_space=pltpu.SMEM)
    dma = pltpu.SemaphoreType.DMA
    call = pl.pallas_call(
        functools.partial(kernel, chips),
        out_shape=(
            jax.ShapeDtypeStruct((rows, poles), jnp.float32),
            jax.ShapeDtypeStruct((cols, poles), jnp.float32),
        ),
        in_specs=[anywhere, vmem, anywhere, vmem, scalar, scalar],
        out_specs=(vmem, vmem),
        scratch_shapes=[
            pltpu.VMEM((chips, poles, cols), jnp.bfloat16),
            pltpu.VMEM((chips, poles, cols), jnp.bfloat16),
            pltpu.VMEM((2, chips, combos, rows, cols), jnp.bfloat16),
            pltpu.VMEM((combos, rows, poles), jnp.bfloat16),
            pltpu.VMEM((poles, rows), jnp.bfloat16),
            pltpu.VMEM((combos, 8, poles), jnp.float32),
            pltpu.VMEM((combos, poles, 128), jnp.float32),
            pltpu.VMEM((combos, rows, poles), jnp.float32),
            pltpu.VMEM((chips, poles, cols), jnp.float32),
            pltpu.VMEM((chips, poles + CODE, cols), jnp.int16),
            pltpu.VMEM((chips, poles + CODE, cols), jnp.int16),
            pltpu.VMEM((chips, PIECES, poles // PIECES + CODE, cols), jnp.int16),
            pltpu.VMEM((chips + 1, PIECES, poles // PIECES + CODE, cols), jnp.int16),
            dma,
            dma((2, chips)),
            dma((chips, PIECES)),
            dma((chips + 1, PIECES)),
            dma((chips,)),
            dma((chips,)),
            dma((chips,)),
            dma((chips,)),
            dma((chips + 1, PIECES)),
            dma((chips + 1, PIECES)),
        ],
        compiler_params=pltpu.CompilerParams(
            collective_id=0, has_side_effects=True, vmem_limit_bytes=60 * 1024 * 1024
        ),
    )
    grad_out, grad_in = call(
        measured.reshape(combos, rows, total_in),
        out_factor,
        in_factor,
        pole_rates.reshape(1, poles),
        freq_index,
        quad_codes,
    )
    return grad_out * (1.0 / math.sqrt(total_in)), grad_in * (1.0 / math.sqrt(total_out))


def plain(measured, out_factor, in_factor, pole_rates, freq_index, quad_codes):
    freq_count = measured.shape[0]
    local_rows, pole_count = out_factor.shape
    local_cols = in_factor.shape[1]
    total_in = measured.shape[3]
    total_out = local_rows * lax.axis_size("port")
    coefficients = pole_terms(freq_index, pole_rates)
    weights = quad_codes.astype(jnp.float32) * 0.25
    weighted = weights[:, None, None] * coefficients
    scaled = (
        out_factor.astype(jnp.float32)[None, None, :, :] * coefficients[:, :, None, :]
    ).astype(jnp.bfloat16)
    block_cols = lax.all_gather(in_factor, "port", axis=1, tiled=True)
    width_cols = block_cols.shape[1]
    model = jnp.dot(scaled.reshape(-1, pole_count), block_cols, preferred_element_type=jnp.float32)
    model = model.reshape(freq_count, 2, local_rows, width_cols)
    residual = (model - measured.astype(jnp.float32)).astype(jnp.bfloat16)
    update = contract_second(residual.reshape(-1, width_cols), block_cols)
    update = update.reshape(freq_count, 2, local_rows, pole_count)
    grad_out = jnp.sum(weighted[:, :, None, :] * update, axis=(0, 1))
    grad_out = grad_out * (1.0 / math.sqrt(total_in))
    running = jnp.zeros((width_cols, pole_count), jnp.float32)
    for freq_slot in range(freq_count):
        for comp_slot in range(2):
            running = running + weighted[freq_slot, comp_slot][None, :] * contract_first(
                residual[freq_slot, comp_slot], out_factor
            )
    grad_in_t = lax.psum_scatter(running, "port", scatter_dimension=0, tiled=True)
    return (grad_out, grad_in_t * (1.0 / math.sqrt(total_out)))


def on_device(measured, out_factor, in_factor, pole_rates, freq_index, quad_codes):
    whole_lanes = in_factor.shape[1] % 128 == 0 and out_factor.shape[1] % 128 == 0
    body = fused if whole_lanes and lax.axis_size("port") % 8 == 0 else plain
    return body(measured, out_factor, in_factor, pole_rates, freq_index, quad_codes)


def solution(mesh):
    in_specs = (
        P("groups", None, "port", None),
        P("port", "groups"),
        P("groups", "port"),
        P("groups"),
        P("groups"),
        P("groups"),
    )
    out_specs = (P("port", "groups"), P("port", "groups"))
    return jax.shard_map(
        on_device, mesh=mesh, in_specs=in_specs, out_specs=out_specs, check_vma=False
    )
```
